128 devices in a mesh: row: 16 (over y, z_hi, core), col: 8 (over z_lo, x).
Axes of the slice: x: 4, y: 4, z: 4 (z_hi: 2, z_lo: 2; z = z_hi * 2 + z_lo), core: 2. Of those that a mesh axis runs over, the one named last changes fastest.
Arguments:
- features: bfloat16 [65536, 256], P('row', 'col'), may hold values from -12 to 12
- tile_vals: bfloat16 [4096, 1024, 128], P('row', 'col'), may hold values from 0 to 4, as said below
- tile_src: int32 [16, 2048], P('row', 'col'), may hold values from 0 to 31
- row_counts: int32 [16, 512], P('row', 'col'), may hold values from 1 to 6, as said below
Outputs:
- propagated: bfloat16 [65536, 256], P(('row', 'col'))
The draws below stay inside these ranges and needn't reach their ends.
Inputs may be any that keep to these rules, and one draw needn't show every extreme that they name: `tile_vals`: each entry is zero or a weight between 0.25 and 4. `row_counts`: on every group the 64 counts sum to at most 256; some groups reach 256 exactly.
All inputs are finite; a program needn't handle non-finite values.
Results may differ from the reference program's by a relative error of at most 0.009.
Values may be sent and summed in bfloat16 or wider, within the bound.
A program may use at most 128 MiB of HBM per device.

```python
import math
import jax
import jax.numpy as jnp
from jax import lax

F = 256
S = 512
TILE = 128
ITERS = 3
DT = 64
ST = 32
TILE_MAX = 256
NODES = 65536
N_ROW = 16
N_COL = 8


def draw_tile_vals(key, part):
    key_edges, key_weights = jax.random.split(key)
    shape_all = (N_ROW * TILE_MAX, N_COL * TILE, TILE)
    edge_mask = jax.random.randint(key_edges, shape_all, 0, TILE) == 0
    weights = jnp.exp(jax.random.uniform(key_weights, shape_all, jnp.float32, math.log(0.25), math.log(4.0)))
    return jnp.where(edge_mask, weights, 0.0).astype(jnp.bfloat16)


def draw_row_counts(key, part):
    devices = N_ROW * N_COL
    half_rows = DT // 2
    key_light, key_base, key_shuffle, key_pick = jax.random.split(key, 4)
    lighter = jax.random.randint(key_light, (devices, DT), 1, 4)
    base_counts = jax.random.randint(key_base, (devices, half_rows), 2, 7)
    heavier = jnp.concatenate([base_counts, 8 - base_counts], axis=1)
    shuffle = jax.vmap(lambda one_key: jax.random.permutation(one_key, DT))(jax.random.split(key_shuffle, devices))
    heavier = jnp.take_along_axis(heavier, shuffle, axis=1)
    ranking = jax.random.permutation(key_pick, devices)
    chosen = (ranking < 4)[:, None]
    counts = jnp.where(chosen, heavier, lighter)
    return counts.reshape(N_ROW, N_COL * DT).astype(jnp.int32)


def place_ends(values, rng, least, top_value):
    longest = values.shape.index(max(values.shape))
    spots = []
    for shift in (0, 1):
        where = [jax.random.randint(jax.random.fold_in(rng, axis), (), 0, length) for axis, length in enumerate(values.shape)]
        where[longest] = (where[longest] + shift) % values.shape[longest]
        spots.append(tuple(where))
    return values.at[spots[0]].set(least).at[spots[1]].set(top_value)


def level_of(own_key, dims, pieces, least, top_value):
    def one(position, shards_of):
        draws = jax.random.uniform(jax.random.fold_in(jax.random.fold_in(own_key, 6), position), (shards_of,), jnp.float32, least / len(pieces), top_value / len(pieces))
        return jnp.repeat(jnp.exp(draws), dims[position] // shards_of).reshape((-1,) + (1,) * (len(dims) - position - 1))

    gain = one(*pieces[0])
    for cut in pieces[1:]:
        gain = gain * one(*cut)
    return gain


def noise(stream_key, dims, deviation, bound, cuts=(), held_as=jnp.bfloat16):
    level = level_of(stream_key, dims, cuts, -0.22, 0.18) if cuts else 1.0
    values = jax.random.normal(stream_key, dims, jnp.float32) * deviation * level
    return jnp.minimum(jnp.maximum(values, -bound), bound).astype(held_as)


def setup_inputs(seed: int = 0) -> dict:
    seeds = jax.random.split(jax.random.key(seed), 5)
    features = noise(seeds[0], (NODES, F), 2.0, 12.0, ((0, 16), (1, 8)))
    tile_vals = draw_tile_vals(jax.random.fold_in(seeds[4], 71), 0)
    tile_src = place_ends(jax.random.randint(seeds[2], (N_ROW, N_COL * TILE_MAX), 0, ST), jax.random.fold_in(seeds[2], 1), 0, ST - 1).astype(jnp.int32)
    row_counts = draw_row_counts(jax.random.fold_in(seeds[4], 71), 0)
    return {"features": features, "tile_vals": tile_vals, "tile_src": tile_src, "row_counts": row_counts}


TELEPORT = 0.1


def slot_layout(counts):
    row_ends = jnp.cumsum(counts, dtype=jnp.int32)
    slot_ids = jnp.arange(TILE_MAX, dtype=jnp.int32)
    dest_tiles = jnp.sum((row_ends[None, :] <= slot_ids[:, None]).astype(jnp.int32), axis=1, dtype=jnp.int32)
    live_slots = slot_ids < row_ends[DT - 1]
    return dest_tiles, live_slots


def group_inputs(group, tile_vals, tile_src, row_counts):
    group = group.astype(jnp.int32)
    row_index = group // N_COL
    col_index = group % N_COL
    tile_block = lax.dynamic_slice_in_dim(tile_vals, (row_index * TILE_MAX).astype(jnp.int32), TILE_MAX, 0)
    tile_block = lax.dynamic_slice_in_dim(tile_block, (col_index * TILE).astype(jnp.int32), TILE, 1)
    src_line = lax.dynamic_index_in_dim(tile_src, row_index, 0, keepdims=False)
    sources = lax.dynamic_slice_in_dim(src_line, (col_index * TILE_MAX).astype(jnp.int32), TILE_MAX, 0)
    count_line = lax.dynamic_index_in_dim(row_counts, row_index, 0, keepdims=False)
    counts = lax.dynamic_slice_in_dim(count_line, (col_index * DT).astype(jnp.int32), DT, 0)
    return row_index, col_index, tile_block, sources, counts


def reference(features, tile_vals, tile_src, row_counts):
    groups = N_ROW * N_COL

    def degree_step(group, running):
        row_index, col_index, tile_block, sources, counts = group_inputs(group, tile_vals, tile_src, row_counts)
        dest_tiles, live_slots = slot_layout(counts)
        column_sums = jnp.sum(tile_block.astype(jnp.float32), axis=1)
        column_sums = jnp.where(live_slots[:, None], column_sums, 0.0)
        weight_sums = jnp.zeros((DT, TILE), jnp.float32).at[dest_tiles].add(column_sums, mode="drop")
        return running.at[:, col_index].add(weight_sums.reshape(N_ROW, S))

    weight_total = lax.fori_loop(0, groups, degree_step, jnp.zeros((N_ROW, N_COL, S), jnp.float32))
    degree = 1.0 + weight_total.reshape(NODES)
    restart = TELEPORT * features.astype(jnp.float32)
    iterate = features
    for iteration in range(ITERS):
        def product_step(group, running, iterate=iterate):
            row_index, col_index, tile_block, sources, counts = group_inputs(group, tile_vals, tile_src, row_counts)
            dest_tiles, live_slots = slot_layout(counts)
            source_rows = lax.dynamic_slice_in_dim(iterate, (row_index * (N_COL * S)).astype(jnp.int32), N_COL * S, 0)
            grouped = source_rows.reshape(ST, TILE, F)
            picked = jnp.take(grouped, sources, axis=0).astype(jnp.float32)
            products = jnp.einsum("tsd,tsf->tdf", tile_block.astype(jnp.float32), picked, precision=lax.Precision.HIGHEST)
            products = jnp.where(live_slots[:, None, None], products, 0.0)
            summed_tiles = jnp.zeros((DT, TILE, F), jnp.float32).at[dest_tiles].add(products, mode="drop")
            rounded = lax.optimization_barrier(summed_tiles.astype(jnp.bfloat16)).astype(jnp.float32)
            return running.at[:, col_index].add(rounded.reshape(N_ROW, S, F))

        summed = lax.fori_loop(0, groups, product_step, jnp.zeros((N_ROW, N_COL, S, F), jnp.float32)).reshape(NODES, F)
        iterate = ((1.0 - TELEPORT) * (summed + iterate.astype(jnp.float32)) / degree[:, None] + restart).astype(jnp.bfloat16)
    return iterate
```

```python
import functools

import jax
import jax.numpy as jnp
from jax import lax
from jax.experimental import pallas as pl
from jax.experimental.pallas import tpu as pltpu
from jax.sharding import PartitionSpec as P

ITERS = 3
TELEPORT = 0.1
TILE = 128
SLOTS = 256
DESTS = 64
SRCS = 32
MOST = 6
FEATS = 256
CHUNKS = 2
WIDE = FEATS // CHUNKS
GROUP = 32 // CHUNKS
TAIL = 16
MESH = pl.DeviceIdType.MESH
F32, BF16 = jnp.float32, jnp.bfloat16


def rows_of(step, chunk):
    return WIDE + (TAIL if (step, chunk) == (0, 0) else 0)


def scratch_layout():
    shapes = {"w": pltpu.VMEM((SLOTS, TILE, TILE), BF16)}
    for k in range(ITERS):
        for ch in range(CHUNKS):
            m = rows_of(k, ch)
            tag = (k, ch)
            shapes["x", tag] = pltpu.VMEM((SRCS + 1, m, TILE), BF16)
            shapes["give", tag] = pltpu.VMEM((8, 4, m, TILE), BF16)
            shapes["take", tag] = pltpu.VMEM((8, 4, m, TILE), BF16)
            shapes["own", tag] = pltpu.VMEM((8, 4, m, TILE), BF16)
            shapes["far_p", tag] = pltpu.VMEM((2, 2, m, TILE), BF16)
            shapes["far_m", tag] = pltpu.VMEM((2, 2, m, TILE), BF16)
            shapes["near_p", tag] = pltpu.VMEM((2, 4, m, TILE), BF16)
            shapes["near_m", tag] = pltpu.VMEM((2, 4, m, TILE), BF16)
            shapes["z_out", tag] = pltpu.VMEM((4, m, TILE), BF16)
            shapes["z_in", tag] = pltpu.VMEM((4, m, TILE), BF16)
            for kind, count in (("core", 8), ("far", 4), ("near", 8), ("z", 1), ("ag", 9)):
                shapes["s_" + kind, tag] = pltpu.SemaphoreType.DMA((count,))
                shapes["r_" + kind, tag] = pltpu.SemaphoreType.DMA((count,))
    shapes["w_sem"] = pltpu.SemaphoreType.DMA((1,))
    shapes["x_sem"] = pltpu.SemaphoreType.DMA((4,))
    shapes["scale"] = pltpu.VMEM((4, 1, TILE), F32)
    shapes["table"] = pltpu.SMEM((DESTS * MOST + DESTS,), jnp.int32)
    return shapes


def kernel(names, src, cnt, feats, w_hbm, out_ref, *scratch):
    ref = dict(zip(names, scratch))
    w, table, scale = ref["w"], ref["table"], ref["scale"]
    row, col = lax.axis_index("row"), lax.axis_index("col")
    core, zh, y = row % 2, (row // 2) % 2, row // 4
    x, zl = col % 4, col // 4
    other_core = (row + 1 - 2 * core, col)
    y_next = (((y + 1) % 4) * 4 + row % 4, col)
    y_prev = (((y + 3) % 4) * 4 + row % 4, col)
    z_far = (row + 2 - 4 * zh, col)
    z_near = (row, col + 4 - 8 * zl)
    x_next = (row, zl * 4 + (x + 1) % 4)
    x_prev = (row, zl * 4 + (x + 3) % 4)
    sends = []

    def remote(kind, tag, index, source, target, device, keep=True):
        copy = pltpu.make_async_remote_copy(
            src_ref=source,
            dst_ref=target,
            send_sem=ref["s_" + kind, tag].at[index],
            recv_sem=ref["r_" + kind, tag].at[index],
            device_id=device,
            device_id_type=MESH,
        )
        copy.start()
        if keep:
            sends.append(copy)

    def arrived(kind, tag, index, target):
        pltpu.make_async_remote_copy(
            src_ref=target,
            dst_ref=target,
            send_sem=ref["s_" + kind, tag].at[index],
            recv_sem=ref["r_" + kind, tag].at[index],
            device_id=other_core,
            device_id_type=MESH,
        ).wait_recv()

    barrier = pltpu.get_barrier_semaphore()
    peers = (other_core, y_next, y_prev, z_far, z_near, x_next, x_prev)
    for peer in peers:
        pl.semaphore_signal(barrier, inc=1, device_id=peer, device_id_type=MESH)
    w_copy = pltpu.make_async_copy(w_hbm, w, ref["w_sem"].at[0])
    loads = []
    for g in range(4):
        ch, part = g // (4 // CHUNKS), g % (4 // CHUNKS)
        first = pl.multiple_of(col * GROUP + part * 8, 8)
        target = ref["x", (0, ch)].at[pl.ds(0, SRCS), pl.ds(first, 8), :]
        loads.append(pltpu.make_async_copy(feats.at[g], target, ref["x_sem"].at[g]))
        loads[-1].start()
    w_copy.start()
    for k in range(ITERS):
        for ch in range(CHUNKS):
            xs = ref["x", (k, ch)]
            xs[SRCS] = jnp.zeros((rows_of(k, ch), TILE), BF16)
    first_row = lax.broadcasted_iota(jnp.int32, (SRCS, TAIL, TILE), 1) == 0
    ref["x", (0, 0)][0:SRCS, WIDE : WIDE + TAIL, :] = jnp.where(first_row, 1.0, 0.0).astype(BF16)
    pl.semaphore_wait(barrier, len(peers))

    def block(k, ch, who, half=None):
        xs = ref["x", (k, ch)]
        if k == 0:
            feat = pl.ds(pl.multiple_of(who * GROUP, GROUP), GROUP)
            if half is None:
                return xs.at[pl.ds(0, SRCS), feat, :]
            return xs.at[pl.ds(half * (SRCS // 2), SRCS // 2), feat, :]
        if half is None:
            return xs.at[pl.ds(who * 4, 4)]
        return xs.at[pl.ds(who * 4 + half * 2, 2)]

    z_col = col + 4 - 8 * zl
    next_col, prev_col = zl * 4 + (x + 1) % 4, zl * 4 + (x + 3) % 4
    far_col = zl * 4 + (x + 2) % 4
    z_next, z_prev = next_col + 4 - 8 * zl, prev_col + 4 - 8 * zl
    z_across = far_col + 4 - 8 * zl

    def gather_0(k, ch):
        mine = block(k, ch, col)
        for index, device in ((0, z_near), (1, x_next), (2, x_prev)):
            remote("ag", (k, ch), index, mine, mine, device)

    def gather_1(k, ch):
        theirs = block(k, ch, z_col)
        arrived("ag", (k, ch), 0, theirs)
        remote("ag", (k, ch), 3, theirs, theirs, x_next)
        remote("ag", (k, ch), 4, theirs, theirs, x_prev)

    def pass_on(k, ch, base, prev_who, next_who):
        arrived("ag", (k, ch), base, block(k, ch, prev_who))
        half = block(k, ch, prev_who, 0)
        remote("ag", (k, ch), base + 4, half, half, x_next)
        arrived("ag", (k, ch), base + 1, block(k, ch, next_who))
        half = block(k, ch, next_who, 1)
        remote("ag", (k, ch), base + 5, half, half, x_prev)

    def gather_2(k, ch):
        pass_on(k, ch, 1, prev_col, next_col)

    def gather_3(k, ch):
        pass_on(k, ch, 3, z_prev, z_next)

    def gather_4(k, ch):
        arrived("ag", (k, ch), 5, block(k, ch, far_col, 0))
        arrived("ag", (k, ch), 6, block(k, ch, far_col, 1))
        arrived("ag", (k, ch), 7, block(k, ch, z_across, 0))
        arrived("ag", (k, ch), 8, block(k, ch, z_across, 1))

    def build_table():
        def one(q, start):
            count = cnt[0, q]
            for j in range(MOST):
                slot = jnp.minimum(start + j, SLOTS - 1)
                table[q * MOST + j] = jnp.where(j < count, src[0, slot], SRCS)
            table[DESTS * MOST + q] = start
            return start + count

        lax.fori_loop(0, DESTS, one, jnp.int32(0))

    def products(k, ch, q):
        xs = ref["x", (k, ch)]
        start = table[DESTS * MOST + q]
        left = jnp.concatenate([xs[table[q * MOST + j]] for j in range(MOST)], axis=1)
        right = jnp.concatenate(
            [w[jnp.minimum(start + j, SLOTS - 1)] for j in range(MOST)], axis=0
        )
        return jnp.dot(left, right, preferred_element_type=F32)

    def tail_sum(terms):
        total = None
        for term in terms:
            part = jnp.sum(term[WIDE:, :].astype(F32), axis=0, keepdims=True)
            total = part if total is None else total + part
        return total

    def add_up(terms):
        total = terms[0][:WIDE, :].astype(F32)
        for term in terms[1:]:
            total = total + term[:WIDE, :].astype(F32)
        return total

    def put(target, terms):
        target[0:WIDE, :] = add_up(terms).astype(BF16)
        if terms[0].shape[0] > WIDE:
            total = tail_sum(terms)
            high = total.astype(BF16).astype(F32)
            low = total - high
            which = lax.broadcasted_iota(jnp.int32, (TAIL, TILE), 0)
            split = jnp.where(which == 0, high, jnp.where(which == 1, low, 0.0))
            target[WIDE : WIDE + TAIL, :] = split.astype(BF16)

    def first_dest(i, side):
        yi = i // 2
        hop = (2 + 3 * yi + 3 * ((yi * (yi - 1)) // 2)) % 4
        z = (1 - zh + i % 2) % 2
        return (((y + hop) % 4) * 4 + z * 2 + side) * 4

    def make_given(k, ch):
        give, take = ref["give", (k, ch)], ref["take", (k, ch)]

        def one(i, carry):
            q = first_dest(i, 1 - core)
            for t in range(4):
                put(give.at[i, t], [products(k, ch, q + t)])
            remote("core", (k, ch), i, give.at[i], take.at[i], other_core, keep=False)
            return carry

        lax.fori_loop(0, 8, one, 0)

    def make_own(k, ch, low, high):
        own, take = ref["own", (k, ch)], ref["take", (k, ch)]

        def one(i, carry):
            q = first_dest(i, core)
            terms = [products(k, ch, q + t) for t in range(4)]
            arrived("core", (k, ch), i, take.at[i])
            for t in range(4):
                put(own.at[i, t], [terms[t], take[i, t]])
            return carry

        lax.fori_loop(low, high, one, 0)

    def own_blocks(k, ch):
        tag = (k, ch)
        own = ref["own", tag]
        make_own(k, ch, 0, 2)
        for zi in range(2):
            remote("far", tag, zi, own.at[zi, 0:2], ref["far_p", tag].at[zi], y_next)
            remote("far", tag, 2 + zi, own.at[zi, 2:4], ref["far_m", tag].at[zi], y_prev)
        make_own(k, ch, 2, 6)
        for zi in range(2):
            remote("near", tag, zi, own.at[2 + zi, 2:4], ref["near_p", tag].at[zi, 2:4], y_next)
            remote("near", tag, 2 + zi, own.at[4 + zi, 0:2], ref["near_m", tag].at[zi, 0:2], y_prev)
        make_own(k, ch, 6, 8)

    def relay(k, ch, zi):
        tag = (k, ch)
        own, far_p, far_m = ref["own", tag], ref["far_p", tag], ref["far_m", tag]
        arrived("far", tag, zi, far_p.at[zi])
        for t in range(2):
            put(own.at[2 + zi, t], [own[2 + zi, t], far_p[zi, t]])
        remote("near", tag, 4 + zi, own.at[2 + zi, 0:2], ref["near_p", tag].at[zi, 0:2], y_next)
        arrived("far", tag, 2 + zi, far_m.at[zi])
        for t in range(2):
            put(own.at[4 + zi, 2 + t], [own[4 + zi, 2 + t], far_m[zi, t]])
        remote("near", tag, 6 + zi, own.at[4 + zi, 2:4], ref["near_m", tag].at[zi, 2:4], y_prev)

    def y_done(k, ch, zi):
        tag = (k, ch)
        arrived("near", tag, zi, ref["near_p", tag].at[zi, 2:4])
        arrived("near", tag, 2 + zi, ref["near_m", tag].at[zi, 0:2])
        arrived("near", tag, 4 + zi, ref["near_p", tag].at[zi, 0:2])
        arrived("near", tag, 6 + zi, ref["near_m", tag].at[zi, 2:4])

    def z_send(k, ch):
        tag = (k, ch)
        y_done(k, ch, 0)
        own, z_out = ref["own", tag], ref["z_out", tag]
        for t in range(4):
            put(z_out.at[t], [own[6, t], ref["near_p", tag][0, t], ref["near_m", tag][0, t]])
        remote("z", tag, 0, z_out, ref["z_in", tag], z_far)

    def finish(k, ch):
        tag = (k, ch)
        y_done(k, ch, 1)
        own, z_in = ref["own", tag], ref["z_in", tag]
        arrived("z", tag, 0, z_in)
        for t in range(4):
            terms = [own[7, t], ref["near_p", tag][1, t], ref["near_m", tag][1, t], z_in[t]]
            if tag == (0, 0):
                scale[t] = (1.0 - TELEPORT) / (1.0 + tail_sum(terms))
            here = col * 4 + t
            old = ref["x", tag][here, 0:WIDE, :].astype(F32)
            start = ref["x", (0, ch)][here, 0:WIDE, :].astype(F32)
            new = ((add_up(terms) + old) * scale[t] + TELEPORT * start).astype(BF16)
            if k + 1 < ITERS:
                ref["x", (k + 1, ch)][here, 0:WIDE, :] = new
            else:
                for g in range(8):
                    low = g * 32 + ch * GROUP
                    out_ref[t, low : low + GROUP, :] = new[g * GROUP : (g + 1) * GROUP, :]
        if k + 1 < ITERS:
            gather_0(k + 1, ch)

    per = 4 // CHUNKS
    for copy in loads[:per]:
        copy.wait()
    gather_0(0, 0)
    build_table()
    gather_1(0, 0)
    gather_2(0, 0)
    gather_3(0, 0)
    for copy in loads[per:]:
        copy.wait()
    gather_0(0, 1)
    gather_4(0, 0)
    w_copy.wait()
    for k in range(ITERS):
        for ch in range(CHUNKS):
            nxt = (k, 1) if ch == 0 else (k + 1, 0)
            busy = nxt[0] < ITERS
            make_given(k, ch)
            if busy:
                gather_1(*nxt)
            own_blocks(k, ch)
            if busy:
                gather_2(*nxt)
            relay(k, ch, 0)
            relay(k, ch, 1)
            if busy:
                gather_3(*nxt)
            z_send(k, ch)
            if busy:
                gather_4(*nxt)
            finish(k, ch)
    for copy in sends:
        copy.wait_send()
    for k in range(ITERS):
        for ch in range(CHUNKS):
            give, take = ref["give", (k, ch)], ref["take", (k, ch)]
            for i in range(8):
                pltpu.make_async_remote_copy(
                    src_ref=give.at[i],
                    dst_ref=take.at[i],
                    send_sem=ref["s_core", (k, ch)].at[i],
                    recv_sem=ref["r_core", (k, ch)].at[i],
                    device_id=other_core,
                    device_id_type=MESH,
                ).wait_send()


def on_device(features, tile_vals, tile_src, row_counts):
    feats = features.T.reshape(4, 8, SRCS, TILE).transpose(0, 2, 1, 3)
    shapes = scratch_layout()
    out = pl.pallas_call(
        functools.partial(kernel, tuple(shapes)),
        out_shape=jax.ShapeDtypeStruct((4, FEATS, TILE), BF16),
        in_specs=[pl.BlockSpec(memory_space=pltpu.SMEM)] * 2
        + [pl.BlockSpec(memory_space=pl.ANY)] * 2,
        out_specs=pl.BlockSpec(memory_space=pltpu.VMEM),
        scratch_shapes=list(shapes.values()),
        compiler_params=pltpu.CompilerParams(
            collective_id=0, has_side_effects=True, vmem_limit_bytes=58 * 2**20
        ),
        name="propagate",
    )(tile_src, row_counts, feats, tile_vals)
    return out.transpose(0, 2, 1).reshape(4 * TILE, FEATS)


def solution(mesh):
    placed = (P("row", "col"), P("row", "col", None), P("row", "col"), P("row", "col"))
    return jax.shard_map(
        on_device, mesh=mesh, in_specs=placed, out_specs=P(("row", "col"), None), check_vma=False
    )
```

```python
import functools

import jax
import jax.numpy as jnp
from jax import lax
from jax.experimental import pallas as pl
from jax.experimental.pallas import tpu as pltpu
from jax.sharding import PartitionSpec as P

ITERS = 3
TELEPORT = 0.1
TILE = 128
SLOTS = 256
DESTS = 64
SRCS = 32
MOST = 6
FEATS = 256
CHUNKS = 4
WIDE = FEATS // CHUNKS
GROUP = 32 // CHUNKS
TAIL = 16
MESH = pl.DeviceIdType.MESH
F32, BF16 = jnp.float32, jnp.bfloat16


def rows_of(step, chunk):
    return WIDE + (TAIL if (step, chunk) == (0, 0) else 0)


def scratch_layout():
    shapes = {"w": pltpu.VMEM((SLOTS, TILE, TILE), BF16)}
    for k in range(ITERS):
        for ch in range(CHUNKS):
            m = rows_of(k, ch)
            tag = (k, ch)
            shapes["x", tag] = pltpu.VMEM((SRCS + 1, m, TILE), BF16)
            shapes["give", tag] = pltpu.VMEM((8, 4, m, TILE), BF16)
            shapes["take", tag] = pltpu.VMEM((8, 4, m, TILE), BF16)
            shapes["own", tag] = pltpu.VMEM((8, 4, m, TILE), BF16)
            shapes["far_p", tag] = pltpu.VMEM((2, 2, m, TILE), BF16)
            shapes["far_m", tag] = pltpu.VMEM((2, 2, m, TILE), BF16)
            shapes["near_p", tag] = pltpu.VMEM((2, 4, m, TILE), BF16)
            shapes["near_m", tag] = pltpu.VMEM((2, 4, m, TILE), BF16)
            shapes["z_out", tag] = pltpu.VMEM((4, m, TILE), BF16)
            shapes["z_in", tag] = pltpu.VMEM((4, m, TILE), BF16)
            for kind, count in (("core", 8), ("far", 4), ("near", 8), ("z", 1), ("ag", 9)):
                shapes["s_" + kind, tag] = pltpu.SemaphoreType.DMA((count,))
                shapes["r_" + kind, tag] = pltpu.SemaphoreType.DMA((count,))
    shapes["w_sem"] = pltpu.SemaphoreType.DMA((1,))
    shapes["x_sem"] = pltpu.SemaphoreType.DMA((4,))
    shapes["scale"] = pltpu.VMEM((4, 1, TILE), F32)
    shapes["table"] = pltpu.SMEM((DESTS * MOST + DESTS,), jnp.int32)
    return shapes


NAMES = (
    "load",
    "weights",
    "gather_0",
    "gather_1",
    "gather_2",
    "gather_3",
    "gather_4",
    "give",
    "own_far",
    "own_rest",
    "relay_0",
    "relay_1",
    "z_send",
    "finish",
)
ORDER = ((2, 0, 0), (2, 0, 1), (2, 0, 2), (4, 0, 0), (3, 0, 0), (3, 0, 1), (3, 0, 2), (5, 0, 0), (4, 0, 1), (5, 0, 1), (4, 0, 2), (2, 0, 3), (5, 0, 2), (1, 0, 0), (0, 0, 2), (0, 0, 1), (0, 0, 0), (0, 0, 3), (6, 0, 0), (7, 0, 0), (6, 0, 1), (3, 0, 3), (7, 0, 1), (8, 0, 0), (6, 0, 2), (7, 0, 2), (8, 0, 1), (5, 0, 3), (4, 0, 3), (9, 0, 0), (10, 0, 0), (9, 0, 1), (10, 0, 1), (8, 0, 2), (6, 0, 3), (7, 0, 3), (12, 0, 0), (11, 0, 0), (9, 0, 2), (12, 0, 1), (11, 0, 1), (8, 0, 3), (10, 0, 2), (9, 0, 3), (13, 0, 0), (2, 1, 0), (10, 0, 3), (13, 0, 1), (2, 1, 1), (11, 0, 2), (12, 0, 2), (3, 1, 0), (4, 1, 0), (12, 0, 3), (3, 1, 1), (4, 1, 1), (11, 0, 3), (5, 1, 0), (13, 0, 2), (2, 1, 2), (5, 1, 1), (13, 0, 3), (2, 1, 3), (6, 1, 0), (7, 1, 0), (3, 1, 2), (4, 1, 2), (6, 1, 1), (7, 1, 1), (8, 1, 0), (3, 1, 3), (9, 1, 0), (5, 1, 2), (4, 1, 3), (8, 1, 1), (9, 1, 1), (10, 1, 0), (5, 1, 3), (11, 1, 0), (6, 1, 2), (7, 1, 2), (10, 1, 1), (11, 1, 1), (6, 1, 3), (7, 1, 3), (12, 1, 0), (8, 1, 2), (12, 1, 1), (9, 1, 2), (8, 1, 3), (10, 1, 2), (9, 1, 3), (13, 1, 0), (2, 2, 0), (13, 1, 1), (10, 1, 3), (2, 2, 1), (12, 1, 2), (3, 2, 0), (11, 1, 3), (11, 1, 2), (12, 1, 3), (4, 2, 0), (3, 2, 1), (4, 2, 1), (5, 2, 0), (13, 1, 2), (2, 2, 2), (5, 2, 1), (13, 1, 3), (6, 2, 0), (2, 2, 3), (7, 2, 0), (3, 2, 2), (4, 2, 2), (6, 2, 1), (7, 2, 1), (3, 2, 3), (8, 2, 0), (9, 2, 0), (5, 2, 2), (4, 2, 3), (8, 2, 1), (9, 2, 1), (5, 2, 3), (10, 2, 0), (11, 2, 0), (6, 2, 2), (7, 2, 2), (10, 2, 1), (6, 2, 3), (7, 2, 3), (8, 2, 2), (9, 2, 2), (12, 2, 1), (8, 2, 3), (12, 2, 0), (10, 2, 2), (9, 2, 3), (10, 2, 3), (11, 2, 3), (11, 2, 2), (11, 2, 1), (12, 2, 2), (12, 2, 3), (13, 2, 1), (13, 2, 0), (13, 2, 2), (13, 2, 3))


def kernel(names, src, cnt, feats, w_hbm, out_ref, *scratch):
    ref = dict(zip(names, scratch))
    w, table, scale = ref["w"], ref["table"], ref["scale"]
    row, col = lax.axis_index("row"), lax.axis_index("col")
    core, zh, y = row % 2, (row // 2) % 2, row // 4
    x, zl = col % 4, col // 4
    other_core = (row + 1 - 2 * core, col)
    y_next = (((y + 1) % 4) * 4 + row % 4, col)
    y_prev = (((y + 3) % 4) * 4 + row % 4, col)
    z_far = (row + 2 - 4 * zh, col)
    z_near = (row, col + 4 - 8 * zl)
    x_next = (row, zl * 4 + (x + 1) % 4)
    x_prev = (row, zl * 4 + (x + 3) % 4)
    sends = []

    def remote(kind, tag, index, source, target, device, keep=True, begin=True):
        copy = pltpu.make_async_remote_copy(
            src_ref=source,
            dst_ref=target,
            send_sem=ref["s_" + kind, tag].at[index],
            recv_sem=ref["r_" + kind, tag].at[index],
            device_id=device,
            device_id_type=MESH,
        )
        if begin:
            copy.start()
        if keep:
            sends.append(copy)

    def arrived(kind, tag, index, target):
        pltpu.make_async_remote_copy(
            src_ref=target,
            dst_ref=target,
            send_sem=ref["s_" + kind, tag].at[index],
            recv_sem=ref["r_" + kind, tag].at[index],
            device_id=other_core,
            device_id_type=MESH,
        ).wait_recv()

    barrier = pltpu.get_barrier_semaphore()
    peers = (other_core, y_next, y_prev, z_far, z_near, x_next, x_prev)
    for peer in peers:
        pl.semaphore_signal(barrier, inc=1, device_id=peer, device_id_type=MESH)
    w_copy = pltpu.make_async_copy(w_hbm, w, ref["w_sem"].at[0])
    loads = []
    for g in range(4):
        ch, part = g // (4 // CHUNKS), g % (4 // CHUNKS)
        first = pl.multiple_of(col * GROUP + part * 8, 8)
        target = ref["x", (0, ch)].at[pl.ds(0, SRCS), pl.ds(first, 8), :]
        loads.append(pltpu.make_async_copy(feats.at[g], target, ref["x_sem"].at[g]))
        loads[-1].start()
    w_copy.start()
    for k in range(ITERS):
        for ch in range(CHUNKS):
            xs = ref["x", (k, ch)]
            xs[SRCS] = jnp.zeros((rows_of(k, ch), TILE), BF16)
    first_row = lax.broadcasted_iota(jnp.int32, (SRCS, TAIL, TILE), 1) == 0
    ref["x", (0, 0)][0:SRCS, WIDE : WIDE + TAIL, :] = jnp.where(first_row, 1.0, 0.0).astype(BF16)

    def build_table():
        def one(q, start):
            count = cnt[0, q]
            for j in range(MOST):
                slot = jnp.minimum(start + j, SLOTS - 1)
                table[q * MOST + j] = jnp.where(j < count, src[0, slot], SRCS)
            table[DESTS * MOST + q] = start
            return start + count

        lax.fori_loop(0, DESTS, one, jnp.int32(0))

    build_table()
    pl.semaphore_wait(barrier, len(peers))

    def block(k, ch, who, half=None):
        xs = ref["x", (k, ch)]
        if k == 0:
            feat = pl.ds(pl.multiple_of(who * GROUP, GROUP), GROUP)
            if half is None:
                return xs.at[pl.ds(0, SRCS), feat, :]
            return xs.at[pl.ds(half * (SRCS // 2), SRCS // 2), feat, :]
        if half is None:
            return xs.at[pl.ds(who * 4, 4)]
        return xs.at[pl.ds(who * 4 + half * 2, 2)]

    z_col = col + 4 - 8 * zl
    next_col, prev_col = zl * 4 + (x + 1) % 4, zl * 4 + (x + 3) % 4
    far_col = zl * 4 + (x + 2) % 4
    z_next, z_prev = next_col + 4 - 8 * zl, prev_col + 4 - 8 * zl
    z_across = far_col + 4 - 8 * zl

    def gather_0(k, ch):
        mine = block(k, ch, col)
        source = mine if k else feats.at[ch]
        for index, device in ((0, z_near), (1, x_next), (2, x_prev)):
            remote("ag", (k, ch), index, source, mine, device)

    def gather_1(k, ch):
        theirs = block(k, ch, z_col)
        arrived("ag", (k, ch), 0, theirs)
        remote("ag", (k, ch), 3, theirs, theirs, x_next)
        remote("ag", (k, ch), 4, theirs, theirs, x_prev)

    def pass_p(k, ch, base, who):
        arrived("ag", (k, ch), base, block(k, ch, who))
        half = block(k, ch, who, 0)
        remote("ag", (k, ch), base + 4, half, half, x_next)

    def pass_m(k, ch, base, who):
        arrived("ag", (k, ch), base + 1, block(k, ch, who))
        half = block(k, ch, who, 1)
        remote("ag", (k, ch), base + 5, half, half, x_prev)

    def gather_2(k, ch):
        pass_p(k, ch, 1, prev_col)
        pass_m(k, ch, 1, next_col)

    def gather_3(k, ch):
        pass_p(k, ch, 3, z_prev)
        pass_m(k, ch, 3, z_next)

    def gather_4(k, ch):
        arrived("ag", (k, ch), 5, block(k, ch, far_col, 0))
        arrived("ag", (k, ch), 6, block(k, ch, far_col, 1))
        arrived("ag", (k, ch), 7, block(k, ch, z_across, 0))
        arrived("ag", (k, ch), 8, block(k, ch, z_across, 1))

    def products(k, ch, q):
        xs = ref["x", (k, ch)]
        start = table[DESTS * MOST + q]
        left = jnp.concatenate([xs[table[q * MOST + j]] for j in range(MOST)], axis=1)
        right = jnp.concatenate(
            [w[jnp.minimum(start + j, SLOTS - 1)] for j in range(MOST)], axis=0
        )
        return jnp.dot(left, right, preferred_element_type=F32)

    def tail_sum(terms):
        total = None
        for term in terms:
            part = jnp.sum(term[WIDE:, :].astype(F32), axis=0, keepdims=True)
            total = part if total is None else total + part
        return total

    def add_up(terms):
        total = terms[0][:WIDE, :].astype(F32)
        for term in terms[1:]:
            total = total + term[:WIDE, :].astype(F32)
        return total

    def put(target, terms):
        target[0:WIDE, :] = add_up(terms).astype(BF16)
        if terms[0].shape[0] > WIDE:
            total = tail_sum(terms)
            high = total.astype(BF16).astype(F32)
            low = total - high
            which = lax.broadcasted_iota(jnp.int32, (TAIL, TILE), 0)
            split = jnp.where(which == 0, high, jnp.where(which == 1, low, 0.0))
            target[WIDE : WIDE + TAIL, :] = split.astype(BF16)

    def first_dest(yi, zi, side):
        hop = (2 + 3 * yi + 3 * ((yi * (yi - 1)) // 2)) % 4
        z = (1 - zh + zi) % 2
        return (((y + hop) % 4) * 4 + z * 2 + side) * 4

    def make_given(k, ch):
        give, take = ref["give", (k, ch)], ref["take", (k, ch)]

        def one(yi, carry):
            sums = [products(k, ch, first_dest(yi, zi, 1 - core) + t) for zi in range(2) for t in range(4)]
            for zi in range(2):
                i = yi * 2 + zi
                for t in range(4):
                    put(give.at[i, t], [sums[zi * 4 + t]])
                remote("core", (k, ch), i, give.at[i], take.at[i], other_core, keep=False)
            return carry

        lax.fori_loop(0, 4, one, 0)

    def make_own(k, ch, yi):
        own, take = ref["own", (k, ch)], ref["take", (k, ch)]
        sums = [products(k, ch, first_dest(yi, zi, core) + t) for zi in range(2) for t in range(4)]
        for zi in range(2):
            i = yi * 2 + zi
            arrived("core", (k, ch), i, take.at[i])
            for t in range(4):
                put(own.at[i, t], [sums[zi * 4 + t], take[i, t]])

    def own_far(k, ch):
        tag = (k, ch)
        own = ref["own", tag]
        make_own(k, ch, 0)
        for zi in range(2):
            remote("far", tag, zi, own.at[zi, 0:2], ref["far_p", tag].at[zi], y_next)
            remote("far", tag, 2 + zi, own.at[zi, 2:4], ref["far_m", tag].at[zi], y_prev)

    def near_p(k, ch, **how):
        tag, own = (k, ch), ref["own", (k, ch)]
        for zi in range(2):
            target = ref["near_p", tag].at[zi, 2:4]
            remote("near", tag, zi, own.at[2 + zi, 2:4], target, y_next, **how)

    def near_m(k, ch, **how):
        tag, own = (k, ch), ref["own", (k, ch)]
        for zi in range(2):
            target = ref["near_m", tag].at[zi, 0:2]
            remote("near", tag, 2 + zi, own.at[4 + zi, 0:2], target, y_prev, **how)

    def own_rest(k, ch):
        def one(yi, carry):
            make_own(k, ch, yi)

            @pl.when(yi == 1)
            def _():
                near_p(k, ch, keep=False)

            @pl.when(yi == 2)
            def _():
                near_m(k, ch, keep=False)

            return carry

        lax.fori_loop(1, 4, one, 0)
        near_p(k, ch, begin=False)
        near_m(k, ch, begin=False)

    def relay(k, ch, zi):
        tag = (k, ch)
        own, far_p, far_m = ref["own", tag], ref["far_p", tag], ref["far_m", tag]
        arrived("far", tag, zi, far_p.at[zi])
        for t in range(2):
            put(own.at[2 + zi, t], [own[2 + zi, t], far_p[zi, t]])
        remote("near", tag, 4 + zi, own.at[2 + zi, 0:2], ref["near_p", tag].at[zi, 0:2], y_next)
        arrived("far", tag, 2 + zi, far_m.at[zi])
        for t in range(2):
            put(own.at[4 + zi, 2 + t], [own[4 + zi, 2 + t], far_m[zi, t]])
        remote("near", tag, 6 + zi, own.at[4 + zi, 2:4], ref["near_m", tag].at[zi, 2:4], y_prev)

    def y_done(k, ch, zi):
        tag = (k, ch)
        arrived("near", tag, zi, ref["near_p", tag].at[zi, 2:4])
        arrived("near", tag, 2 + zi, ref["near_m", tag].at[zi, 0:2])
        arrived("near", tag, 4 + zi, ref["near_p", tag].at[zi, 0:2])
        arrived("near", tag, 6 + zi, ref["near_m", tag].at[zi, 2:4])

    def relay_0(k, ch):
        relay(k, ch, 0)

    def relay_1(k, ch):
        relay(k, ch, 1)

    def z_send(k, ch):
        tag = (k, ch)
        y_done(k, ch, 0)
        own, z_out = ref["own", tag], ref["z_out", tag]
        for t in range(4):
            put(z_out.at[t], [own[6, t], ref["near_p", tag][0, t], ref["near_m", tag][0, t]])
        remote("z", tag, 0, z_out, ref["z_in", tag], z_far)

    def finish(k, ch):
        tag = (k, ch)
        y_done(k, ch, 1)
        own, z_in = ref["own", tag], ref["z_in", tag]
        arrived("z", tag, 0, z_in)
        for t in range(4):
            terms = [own[7, t], ref["near_p", tag][1, t], ref["near_m", tag][1, t], z_in[t]]
            if tag == (0, 0):
                scale[t] = (1.0 - TELEPORT) / (1.0 + tail_sum(terms))
            here = col * 4 + t
            old = ref["x", tag][here, 0:WIDE, :].astype(F32)
            start = ref["x", (0, ch)][here, 0:WIDE, :].astype(F32)
            new = ((add_up(terms) + old) * scale[t] + TELEPORT * start).astype(BF16)
            if k + 1 < ITERS:
                ref["x", (k + 1, ch)][here, 0:WIDE, :] = new
            else:
                for g in range(8):
                    low = g * 32 + ch * GROUP
                    out_ref[t, low : low + GROUP, :] = new[g * GROUP : (g + 1) * GROUP, :]
    def load(k, ch):
        loads[ch].wait()

    def weights(k, ch):
        w_copy.wait()

    tasks = dict(
        load=load,
        weights=weights,
        gather_0=gather_0,
        gather_1=gather_1,
        gather_2=gather_2,
        gather_3=gather_3,
        gather_4=gather_4,
        give=make_given,
        own_far=own_far,
        own_rest=own_rest,
        relay_0=relay_0,
        relay_1=relay_1,
        z_send=z_send,
        finish=finish,
    )
    for number, k, ch in ORDER:
        tasks[NAMES[number]](k, ch)
    for copy in sends:
        copy.wait_send()
    for k in range(ITERS):
        for ch in range(CHUNKS):
            give, take = ref["give", (k, ch)], ref["take", (k, ch)]
            for i in range(8):
                pltpu.make_async_remote_copy(
                    src_ref=give.at[i],
                    dst_ref=take.at[i],
                    send_sem=ref["s_core", (k, ch)].at[i],
                    recv_sem=ref["r_core", (k, ch)].at[i],
                    device_id=other_core,
                    device_id_type=MESH,
                ).wait_send()


def on_device(features, tile_vals, tile_src, row_counts):
    feats = features.T.reshape(4, 8, SRCS, TILE).transpose(0, 2, 1, 3)
    shapes = scratch_layout()
    out = pl.pallas_call(
        functools.partial(kernel, tuple(shapes)),
        out_shape=jax.ShapeDtypeStruct((4, FEATS, TILE), BF16),
        in_specs=[pl.BlockSpec(memory_space=pltpu.SMEM)] * 2
        + [pl.BlockSpec(memory_space=pl.ANY)] * 2,
        out_specs=pl.BlockSpec(memory_space=pltpu.VMEM),
        scratch_shapes=list(shapes.values()),
        compiler_params=pltpu.CompilerParams(
            collective_id=0, has_side_effects=True, vmem_limit_bytes=58 * 2**20
        ),
        name="propagate",
    )(tile_src, row_counts, feats, tile_vals)
    return out.transpose(0, 2, 1).reshape(4 * TILE, FEATS)


def solution(mesh):
    placed = (P("row", "col"), P("row", "col", None), P("row", "col"), P("row", "col"))
    return jax.shard_map(
        on_device, mesh=mesh, in_specs=placed, out_specs=P(("row", "col"), None), check_vma=False
    )
```

```python
import functools

import jax
import jax.numpy as jnp
from jax import lax
from jax.experimental import pallas as pl
from jax.experimental.pallas import tpu as pltpu
from jax.sharding import PartitionSpec as P

ITERS = 3
TELEPORT = 0.1
TILE = 128
SLOTS = 256
DESTS = 64
SRCS = 32
MOST = 6
FEATS = 256
CHUNKS = 4
WIDE = FEATS // CHUNKS
GROUP = 32 // CHUNKS
TAIL = 16
MESH = pl.DeviceIdType.MESH
F32, BF16 = jnp.float32, jnp.bfloat16


def rows_of(step, chunk):
    return WIDE + (TAIL if (step, chunk) == (0, 0) else 0)


def scratch_layout():
    shapes = {"w": pltpu.VMEM((SLOTS, TILE, TILE), BF16)}
    for k in range(ITERS):
        for ch in range(CHUNKS):
            m = rows_of(k, ch)
            tag = (k, ch)
            shapes["x", tag] = pltpu.VMEM((SRCS + 1, m, TILE), BF16)
            shapes["give", tag] = pltpu.VMEM((8, 4, m, TILE), BF16)
            shapes["take", tag] = pltpu.VMEM((8, 4, m, TILE), BF16)
            shapes["own", tag] = pltpu.VMEM((8, 4, m, TILE), BF16)
            shapes["far", tag] = pltpu.VMEM((2, 4, m, TILE), BF16)
            shapes["near_p", tag] = pltpu.VMEM((2, 4, m, TILE), BF16)
            shapes["near_m", tag] = pltpu.VMEM((2, 4, m, TILE), BF16)
            shapes["z_out", tag] = pltpu.VMEM((4, m, TILE), BF16)
            shapes["z_in", tag] = pltpu.VMEM((4, m, TILE), BF16)
            for kind, count in (("core", 4), ("y", 6), ("z", 1), ("ag", 9)):
                shapes["s_" + kind, tag] = pltpu.SemaphoreType.DMA((count,))
                shapes["r_" + kind, tag] = pltpu.SemaphoreType.DMA((count,))
    shapes["w_sem"] = pltpu.SemaphoreType.DMA((1,))
    shapes["x_sem"] = pltpu.SemaphoreType.DMA((4,))
    shapes["scale"] = pltpu.VMEM((4, 1, TILE), F32)
    shapes["table"] = pltpu.SMEM((DESTS * MOST + DESTS,), jnp.int32)
    return shapes


NAMES = (
    "load",
    "weights",
    "gather_0",
    "gather_1",
    "gather_2",
    "gather_3",
    "gather_4",
    "give",
    "own_0",
    "own_1",
    "z_send",
    "finish",
    "drain",
)
ORDER = ((2, 0, 0), (2, 0, 1), (2, 0, 2), (3, 0, 0), (4, 0, 0), (3, 0, 2), (0, 0, 2), (1, 0, 0), (5, 0, 0), (4, 0, 2), (4, 0, 1), (5, 0, 2), (3, 0, 1), (2, 0, 3), (0, 0, 0), (6, 0, 0), (7, 0, 0), (6, 0, 2), (7, 0, 2), (8, 0, 0), (3, 0, 3), (9, 0, 0), (8, 0, 2), (9, 0, 2), (4, 0, 3), (5, 0, 1), (10, 0, 0), (5, 0, 3), (0, 0, 1), (0, 0, 3), (6, 0, 1), (7, 0, 1), (6, 0, 3), (11, 0, 0), (2, 1, 0), (10, 0, 2), (8, 0, 1), (7, 0, 3), (3, 1, 0), (9, 0, 1), (11, 0, 2), (2, 1, 2), (10, 0, 1), (8, 0, 3), (9, 0, 3), (6, 1, 0), (3, 1, 2), (7, 1, 0), (11, 0, 1), (2, 1, 1), (10, 0, 3), (8, 1, 0), (9, 1, 0), (6, 1, 2), (3, 1, 1), (7, 1, 2), (11, 0, 3), (2, 1, 3), (10, 1, 0), (8, 1, 2), (6, 1, 1), (7, 1, 1), (3, 1, 3), (9, 1, 2), (11, 1, 0), (2, 2, 0), (10, 1, 2), (8, 1, 1), (9, 1, 1), (6, 1, 3), (3, 2, 0), (7, 1, 3), (11, 1, 2), (10, 1, 1), (2, 2, 2), (8, 1, 3), (6, 2, 0), (7, 2, 0), (3, 2, 2), (11, 1, 1), (2, 2, 1), (9, 1, 3), (10, 1, 3), (8, 2, 0), (9, 2, 0), (3, 2, 1), (6, 2, 2), (7, 2, 2), (11, 1, 3), (2, 2, 3), (12, 1, 1), (8, 2, 2), (9, 2, 2), (6, 2, 1), (3, 2, 3), (7, 2, 1), (12, 0, 3), (12, 0, 0), (8, 2, 1), (6, 2, 3), (7, 2, 3), (9, 2, 1), (10, 2, 2), (10, 2, 0), (12, 1, 2), (8, 2, 3), (9, 2, 3), (12, 1, 0), (10, 2, 1), (12, 1, 3), (11, 2, 2), (12, 0, 2), (11, 2, 0), (10, 2, 3), (11, 2, 1), (12, 0, 1), (12, 2, 2), (12, 2, 0), (12, 2, 1), (11, 2, 3), (12, 2, 3))


def kernel(names, src, cnt, feats, w_hbm, out_ref, *scratch):
    ref = dict(zip(names, scratch))
    w, table, scale = ref["w"], ref["table"], ref["scale"]
    row, col = lax.axis_index("row"), lax.axis_index("col")
    core, zh, y = row % 2, (row // 2) % 2, row // 4
    x, zl = col % 4, col // 4
    other_core = (row + 1 - 2 * core, col)
    y_next = (((y + 1) % 4) * 4 + row % 4, col)
    y_far = (((y + 2) % 4) * 4 + row % 4, col)
    y_prev = (((y + 3) % 4) * 4 + row % 4, col)
    z_far = (row + 2 - 4 * zh, col)
    z_near = (row, col + 4 - 8 * zl)
    x_next = (row, zl * 4 + (x + 1) % 4)
    x_far = (row, zl * 4 + (x + 2) % 4)
    x_prev = (row, zl * 4 + (x + 3) % 4)
    sends = {(k, ch): [] for k in range(ITERS) for ch in range(CHUNKS)}

    def remote(kind, tag, index, source, target, device, keep=True, begin=True):
        copy = pltpu.make_async_remote_copy(
            src_ref=source,
            dst_ref=target,
            send_sem=ref["s_" + kind, tag].at[index],
            recv_sem=ref["r_" + kind, tag].at[index],
            device_id=device,
            device_id_type=MESH,
        )
        if begin:
            copy.start()
        if keep:
            sends[tag].append(copy)

    def arrived(kind, tag, index, target):
        pltpu.make_async_remote_copy(
            src_ref=target,
            dst_ref=target,
            send_sem=ref["s_" + kind, tag].at[index],
            recv_sem=ref["r_" + kind, tag].at[index],
            device_id=other_core,
            device_id_type=MESH,
        ).wait_recv()

    barrier = pltpu.get_barrier_semaphore()
    peers = (other_core, y_next, y_prev, y_far, z_far, z_near, x_next, x_prev, x_far)
    for peer in peers:
        pl.semaphore_signal(barrier, inc=1, device_id=peer, device_id_type=MESH)
    w_copy = pltpu.make_async_copy(w_hbm, w, ref["w_sem"].at[0])
    loads = []
    for g in range(4):
        ch, part = g // (4 // CHUNKS), g % (4 // CHUNKS)
        first = pl.multiple_of(col * GROUP + part * 8, 8)
        target = ref["x", (0, ch)].at[pl.ds(0, SRCS), pl.ds(first, 8), :]
        loads.append(pltpu.make_async_copy(feats.at[g], target, ref["x_sem"].at[g]))
        loads[-1].start()
    w_copy.start()
    for k in range(ITERS):
        for ch in range(CHUNKS):
            xs = ref["x", (k, ch)]
            xs[SRCS] = jnp.zeros((rows_of(k, ch), TILE), BF16)
    first_row = lax.broadcasted_iota(jnp.int32, (SRCS, TAIL, TILE), 1) == 0
    ref["x", (0, 0)][0:SRCS, WIDE : WIDE + TAIL, :] = jnp.where(first_row, 1.0, 0.0).astype(BF16)

    def build_table():
        def one(q, start):
            count = cnt[0, q]
            for j in range(MOST):
                slot = jnp.minimum(start + j, SLOTS - 1)
                table[q * MOST + j] = jnp.where(j < count, src[0, slot], SRCS)
            table[DESTS * MOST + q] = start
            return start + count

        lax.fori_loop(0, DESTS, one, jnp.int32(0))

    build_table()
    pl.semaphore_wait(barrier, len(peers))

    def block(k, ch, who, half=None):
        xs = ref["x", (k, ch)]
        if k == 0:
            feat = pl.ds(pl.multiple_of(who * GROUP, GROUP), GROUP)
            if half is None:
                return xs.at[pl.ds(0, SRCS), feat, :]
            return xs.at[pl.ds(half * (SRCS // 2), SRCS // 2), feat, :]
        if half is None:
            return xs.at[pl.ds(who * 4, 4)]
        return xs.at[pl.ds(who * 4 + half * 2, 2)]

    z_col = col + 4 - 8 * zl
    next_col, prev_col = zl * 4 + (x + 1) % 4, zl * 4 + (x + 3) % 4
    far_col = zl * 4 + (x + 2) % 4
    z_next, z_prev = next_col + 4 - 8 * zl, prev_col + 4 - 8 * zl
    z_across = far_col + 4 - 8 * zl

    def gather_0(k, ch):
        mine = block(k, ch, col)
        source = mine if k else feats.at[ch]
        remote("ag", (k, ch), 0, source, mine, z_near)
        if k:
            remote("ag", (k, ch), 3, source, mine, x_far)
        remote("ag", (k, ch), 1, source, mine, x_next)
        remote("ag", (k, ch), 2, source, mine, x_prev)

    def gather_1(k, ch):
        theirs = block(k, ch, z_col)
        arrived("ag", (k, ch), 0, theirs)
        if k:
            remote("ag", (k, ch), 6, theirs, theirs, x_far)
            remote("ag", (k, ch), 4, theirs, theirs, x_next)
            remote("ag", (k, ch), 5, theirs, theirs, x_prev)
        else:
            remote("ag", (k, ch), 3, theirs, theirs, x_next)
            remote("ag", (k, ch), 4, theirs, theirs, x_prev)

    def pass_p(k, ch, base, who):
        arrived("ag", (k, ch), base, block(k, ch, who))
        half = block(k, ch, who, 0)
        remote("ag", (k, ch), base + 4, half, half, x_next)

    def pass_m(k, ch, base, who):
        arrived("ag", (k, ch), base + 1, block(k, ch, who))
        half = block(k, ch, who, 1)
        remote("ag", (k, ch), base + 5, half, half, x_prev)

    def gather_2(k, ch):
        pass_p(k, ch, 1, prev_col)
        pass_m(k, ch, 1, next_col)

    def gather_3(k, ch):
        pass_p(k, ch, 3, z_prev)
        pass_m(k, ch, 3, z_next)

    def gather_4(k, ch):
        if k:
            who = (prev_col, next_col, far_col, z_prev, z_next, z_across)
            for i in range(6):
                arrived("ag", (k, ch), i + 1, block(k, ch, who[i]))
        else:
            arrived("ag", (k, ch), 5, block(k, ch, far_col, 0))
            arrived("ag", (k, ch), 6, block(k, ch, far_col, 1))
            arrived("ag", (k, ch), 7, block(k, ch, z_across, 0))
            arrived("ag", (k, ch), 8, block(k, ch, z_across, 1))

    def products(k, ch, q):
        xs = ref["x", (k, ch)]
        start = table[DESTS * MOST + q]
        left = jnp.concatenate([xs[table[q * MOST + j]] for j in range(MOST)], axis=1)
        right = jnp.concatenate(
            [w[jnp.minimum(start + j, SLOTS - 1)] for j in range(MOST)], axis=0
        )
        return jnp.dot(left, right, preferred_element_type=F32)

    def tail_sum(terms):
        total = None
        for term in terms:
            part = jnp.sum(term[WIDE:, :].astype(F32), axis=0, keepdims=True)
            total = part if total is None else total + part
        return total

    def add_up(terms):
        total = terms[0][:WIDE, :].astype(F32)
        for term in terms[1:]:
            total = total + term[:WIDE, :].astype(F32)
        return total

    def put(target, terms):
        target[0:WIDE, :] = add_up(terms).astype(BF16)
        if terms[0].shape[0] > WIDE:
            total = tail_sum(terms)
            high = total.astype(BF16).astype(F32)
            low = total - high
            which = lax.broadcasted_iota(jnp.int32, (TAIL, TILE), 0)
            split = jnp.where(which == 0, high, jnp.where(which == 1, low, 0.0))
            target[WIDE : WIDE + TAIL, :] = split.astype(BF16)

    def first_dest(i, side):
        zi, yi = i // 4, i % 4
        hop = (2 + 3 * yi + 3 * ((yi * (yi - 1)) // 2)) % 4
        z = (1 - zh + zi) % 2
        return (((y + hop) % 4) * 4 + z * 2 + side) * 4

    def core_copy(k, ch, pair, **how):
        give, take = ref["give", (k, ch)], ref["take", (k, ch)]
        both = pl.ds(pair * 2, 2)
        remote("core", (k, ch), pair, give.at[both], take.at[both], other_core, **how)

    def make_given(k, ch):
        give = ref["give", (k, ch)]

        def one(pair, carry):
            sums = [products(k, ch, first_dest(pair * 2 + e, 1 - core) + t) for e in range(2) for t in range(4)]
            for e in range(2):
                for t in range(4):
                    put(give.at[pair * 2 + e, t], [sums[e * 4 + t]])
            core_copy(k, ch, pair, keep=False)
            return carry

        lax.fori_loop(0, 4, one, 0)
        for pair in range(4):
            core_copy(k, ch, pair, begin=False)

    def y_first(k, ch, zi, **how):
        tag, own = (k, ch), ref["own", (k, ch)]
        remote("y", tag, zi * 3, own.at[zi * 4], ref["far", tag].at[zi], y_far, **how)
        remote("y", tag, zi * 3 + 1, own.at[zi * 4 + 1], ref["near_p", tag].at[zi], y_next, **how)

    def y_second(k, ch, zi, **how):
        tag, own = (k, ch), ref["own", (k, ch)]
        remote("y", tag, zi * 3 + 2, own.at[zi * 4 + 2], ref["near_m", tag].at[zi], y_prev, **how)

    def make_own(k, ch, zi):
        own, take = ref["own", (k, ch)], ref["take", (k, ch)]

        def one(h, carry):
            pair = zi * 2 + h
            sums = [products(k, ch, first_dest(pair * 2 + e, core) + t) for e in range(2) for t in range(4)]
            arrived("core", (k, ch), pair, take.at[pl.ds(pair * 2, 2)])
            for e in range(2):
                i = pair * 2 + e
                for t in range(4):
                    put(own.at[i, t], [sums[e * 4 + t], take[i, t]])

            @pl.when(h == 0)
            def _():
                y_first(k, ch, zi, keep=False)

            @pl.when(h == 1)
            def _():
                y_second(k, ch, zi, keep=False)

            return carry

        lax.fori_loop(0, 2, one, 0)
        y_first(k, ch, zi, begin=False)
        y_second(k, ch, zi, begin=False)

    def own_0(k, ch):
        make_own(k, ch, 0)

    def own_1(k, ch):
        make_own(k, ch, 1)

    def y_terms(k, ch, zi):
        buffers = [ref[name, (k, ch)] for name in ("far", "near_p", "near_m")]
        for i, buffer in enumerate(buffers):
            arrived("y", (k, ch), zi * 3 + i, buffer.at[zi])
        own = ref["own", (k, ch)]
        return [[own[zi * 4 + 3, t]] + [buffer[zi, t] for buffer in buffers] for t in range(4)]

    def z_send(k, ch):
        tag = (k, ch)
        z_out = ref["z_out", tag]
        terms = y_terms(k, ch, 0)
        for t in range(4):
            put(z_out.at[t], terms[t])
        remote("z", tag, 0, z_out, ref["z_in", tag], z_far)

    def finish(k, ch):
        tag = (k, ch)
        z_in = ref["z_in", tag]
        sums = y_terms(k, ch, 1)
        arrived("z", tag, 0, z_in)
        for t in range(4):
            terms = sums[t] + [z_in[t]]
            if tag == (0, 0):
                scale[t] = (1.0 - TELEPORT) / (1.0 + tail_sum(terms))
            here = col * 4 + t
            old = ref["x", tag][here, 0:WIDE, :].astype(F32)
            start = ref["x", (0, ch)][here, 0:WIDE, :].astype(F32)
            new = ((add_up(terms) + old) * scale[t] + TELEPORT * start).astype(BF16)
            if k + 1 < ITERS:
                ref["x", (k + 1, ch)][here, 0:WIDE, :] = new
            else:
                for g in range(8):
                    low = g * 32 + ch * GROUP
                    out_ref[t, low : low + GROUP, :] = new[g * GROUP : (g + 1) * GROUP, :]

    def drain(k, ch):
        for copy in sends[k, ch]:
            copy.wait_send()

    def load(k, ch):
        loads[ch].wait()

    def weights(k, ch):
        w_copy.wait()

    tasks = dict(
        load=load,
        weights=weights,
        gather_0=gather_0,
        gather_1=gather_1,
        gather_2=gather_2,
        gather_3=gather_3,
        gather_4=gather_4,
        give=make_given,
        own_0=own_0,
        own_1=own_1,
        z_send=z_send,
        finish=finish,
        drain=drain,
    )
    for number, k, ch in ORDER:
        tasks[NAMES[number]](k, ch)

def on_device(features, tile_vals, tile_src, row_counts):
    feats = features.T.reshape(4, 8, SRCS, TILE).transpose(0, 2, 1, 3)
    shapes = scratch_layout()
    out = pl.pallas_call(
        functools.partial(kernel, tuple(shapes)),
        out_shape=jax.ShapeDtypeStruct((4, FEATS, TILE), BF16),
        in_specs=[pl.BlockSpec(memory_space=pltpu.SMEM)] * 2
        + [pl.BlockSpec(memory_space=pl.ANY)] * 2,
        out_specs=pl.BlockSpec(memory_space=pltpu.VMEM),
        scratch_shapes=list(shapes.values()),
        compiler_params=pltpu.CompilerParams(
            collective_id=0, has_side_effects=True, vmem_limit_bytes=58 * 2**20
        ),
        name="propagate",
    )(tile_src, row_counts, feats, tile_vals)
    return out.transpose(0, 2, 1).reshape(4 * TILE, FEATS)


def solution(mesh):
    placed = (P("row", "col"), P("row", "col", None), P("row", "col"), P("row", "col"))
    return jax.shard_map(
        on_device, mesh=mesh, in_specs=placed, out_specs=P(("row", "col"), None), check_vma=False
    )
```

```python
import functools

import jax
import jax.numpy as jnp
from jax import lax
from jax.experimental import pallas as pl
from jax.experimental.pallas import tpu as pltpu
from jax.sharding import PartitionSpec as P

ITERS = 3
TELEPORT = 0.1
TILE = 128
SLOTS = 256
DESTS = 64
SRCS = 32
MOST = 6
FEATS = 256
CHUNKS = 4
WIDE = FEATS // CHUNKS
GROUP = 32 // CHUNKS
TAIL = 16
MESH = pl.DeviceIdType.MESH
F32, BF16 = jnp.float32, jnp.bfloat16


def rows_of(step, chunk):
    return WIDE + (TAIL if (step, chunk) == (0, 0) else 0)


def scratch_layout():
    shapes = {"w": pltpu.VMEM((SLOTS, TILE, TILE), BF16)}
    for k in range(ITERS):
        for ch in range(CHUNKS):
            m = rows_of(k, ch)
            tag = (k, ch)
            shapes["x", tag] = pltpu.VMEM((SRCS + 1, m, TILE), BF16)
            shapes["give", tag] = pltpu.VMEM((8, 4, m, TILE), BF16)
            shapes["take", tag] = pltpu.VMEM((8, 4, m, TILE), BF16)
            shapes["own", tag] = pltpu.VMEM((8, 4, m, TILE), BF16)
            shapes["far", tag] = pltpu.VMEM((2, 4, m, TILE), BF16)
            shapes["near_p", tag] = pltpu.VMEM((2, 4, m, TILE), BF16)
            shapes["near_m", tag] = pltpu.VMEM((2, 4, m, TILE), BF16)
            shapes["z_out", tag] = pltpu.VMEM((4, m, TILE), BF16)
            shapes["z_in", tag] = pltpu.VMEM((4, m, TILE), BF16)
            for kind, count in (("core", 4), ("y", 6), ("z", 1), ("ag", 9)):
                shapes["s_" + kind, tag] = pltpu.SemaphoreType.DMA((count,))
                shapes["r_" + kind, tag] = pltpu.SemaphoreType.DMA((count,))
    shapes["w_sem"] = pltpu.SemaphoreType.DMA((1,))
    shapes["x_sem"] = pltpu.SemaphoreType.DMA((4,))
    shapes["scale"] = pltpu.VMEM((4, 1, TILE), F32)
    shapes["table"] = pltpu.SMEM((DESTS * MOST + DESTS,), jnp.int32)
    return shapes


NAMES = (
    "load",
    "weights",
    "gather_0",
    "gather_1",
    "gather_2",
    "gather_3",
    "gather_4",
    "give",
    "own_0",
    "own_1",
    "z_send",
    "finish",
    "drain",
)
ORDER = ((2, 0, 0), (2, 0, 2), (2, 0, 1), (4, 0, 0), (3, 0, 0), (3, 0, 1), (3, 0, 2), (5, 0, 0), (4, 0, 1), (0, 0, 1), (0, 0, 0), (5, 0, 1), (2, 0, 3), (5, 0, 2), (0, 0, 2), (1, 0, 0), (4, 0, 2), (6, 0, 0), (7, 0, 0), (6, 0, 1), (7, 0, 1), (8, 0, 0), (9, 0, 0), (3, 0, 3), (4, 0, 3), (0, 0, 3), (6, 0, 2), (7, 0, 2), (8, 0, 1), (10, 0, 0), (9, 0, 1), (5, 0, 3), (6, 0, 3), (11, 0, 0), (2, 1, 0), (10, 0, 1), (8, 0, 2), (7, 0, 3), (3, 1, 0), (9, 0, 2), (11, 0, 1), (2, 1, 1), (10, 0, 2), (8, 0, 3), (9, 0, 3), (6, 1, 0), (3, 1, 1), (7, 1, 0), (11, 0, 2), (2, 1, 2), (10, 0, 3), (8, 1, 0), (9, 1, 0), (6, 1, 1), (3, 1, 2), (7, 1, 1), (11, 0, 3), (2, 1, 3), (10, 1, 0), (8, 1, 1), (6, 1, 2), (7, 1, 2), (3, 1, 3), (9, 1, 1), (11, 1, 0), (2, 2, 0), (12, 1, 0), (10, 1, 1), (8, 1, 2), (9, 1, 2), (6, 1, 3), (3, 2, 0), (7, 1, 3), (11, 1, 1), (2, 2, 1), (10, 1, 2), (8, 1, 3), (9, 1, 3), (6, 2, 0), (3, 2, 1), (7, 2, 0), (11, 1, 2), (2, 2, 2), (12, 1, 2), (10, 1, 3), (8, 2, 0), (6, 2, 1), (9, 2, 0), (3, 2, 2), (7, 2, 1), (11, 1, 3), (2, 2, 3), (8, 2, 1), (6, 2, 2), (7, 2, 2), (3, 2, 3), (9, 2, 1), (12, 0, 3), (8, 2, 2), (10, 2, 1), (9, 2, 2), (10, 2, 0), (6, 2, 3), (7, 2, 3), (12, 0, 1), (8, 2, 3), (11, 2, 1), (11, 2, 0), (12, 0, 0), (10, 2, 2), (12, 1, 3), (9, 2, 3), (10, 2, 3), (12, 2, 0), (12, 2, 1), (12, 0, 2), (11, 2, 2), (12, 1, 1), (12, 2, 2), (11, 2, 3), (12, 2, 3))


def kernel(names, src, cnt, feats, w_hbm, out_ref, *scratch):
    ref = dict(zip(names, scratch))
    w, table, scale = ref["w"], ref["table"], ref["scale"]
    row, col = lax.axis_index("row"), lax.axis_index("col")
    core, zh, y = row % 2, (row // 2) % 2, row // 4
    x, zl = col % 4, col // 4
    other_core = (row + 1 - 2 * core, col)
    y_next = (((y + 1) % 4) * 4 + row % 4, col)
    y_far = (((y + 2) % 4) * 4 + row % 4, col)
    y_prev = (((y + 3) % 4) * 4 + row % 4, col)
    z_far = (row + 2 - 4 * zh, col)
    z_near = (row, col + 4 - 8 * zl)
    x_next = (row, zl * 4 + (x + 1) % 4)
    x_far = (row, zl * 4 + (x + 2) % 4)
    x_prev = (row, zl * 4 + (x + 3) % 4)
    sends = {(k, ch): [] for k in range(ITERS) for ch in range(CHUNKS)}

    def remote(kind, tag, index, source, target, device, keep=True, begin=True):
        copy = pltpu.make_async_remote_copy(
            src_ref=source,
            dst_ref=target,
            send_sem=ref["s_" + kind, tag].at[index],
            recv_sem=ref["r_" + kind, tag].at[index],
            device_id=device,
            device_id_type=MESH,
        )
        if begin:
            copy.start()
        if keep:
            sends[tag].append(copy)

    def arrived(kind, tag, index, target):
        pltpu.make_async_remote_copy(
            src_ref=target,
            dst_ref=target,
            send_sem=ref["s_" + kind, tag].at[index],
            recv_sem=ref["r_" + kind, tag].at[index],
            device_id=other_core,
            device_id_type=MESH,
        ).wait_recv()

    barrier = pltpu.get_barrier_semaphore()
    peers = (other_core, y_next, y_prev, y_far, z_far, z_near, x_next, x_prev, x_far)
    for peer in peers:
        pl.semaphore_signal(barrier, inc=1, device_id=peer, device_id_type=MESH)
    w_copy = pltpu.make_async_copy(w_hbm, w, ref["w_sem"].at[0])
    loads = []
    for g in range(4):
        ch, part = g // (4 // CHUNKS), g % (4 // CHUNKS)
        first = pl.multiple_of(col * GROUP + part * 8, 8)
        target = ref["x", (0, ch)].at[pl.ds(0, SRCS), pl.ds(first, 8), :]
        loads.append(pltpu.make_async_copy(feats.at[g], target, ref["x_sem"].at[g]))
        loads[-1].start()
    w_copy.start()
    for k in range(ITERS):
        for ch in range(CHUNKS):
            xs = ref["x", (k, ch)]
            xs[SRCS] = jnp.zeros((rows_of(k, ch), TILE), BF16)
    first_row = lax.broadcasted_iota(jnp.int32, (SRCS, TAIL, TILE), 1) == 0
    ref["x", (0, 0)][0:SRCS, WIDE : WIDE + TAIL, :] = jnp.where(first_row, 1.0, 0.0).astype(BF16)

    def build_table():
        def one(q, start):
            count = cnt[0, q]
            for j in range(MOST):
                slot = jnp.minimum(start + j, SLOTS - 1)
                table[q * MOST + j] = jnp.where(j < count, src[0, slot], SRCS)
            table[DESTS * MOST + q] = start
            return start + count

        lax.fori_loop(0, DESTS, one, jnp.int32(0))

    build_table()
    pl.semaphore_wait(barrier, len(peers))

    def block(k, ch, who, half=None):
        xs = ref["x", (k, ch)]
        if k == 0:
            feat = pl.ds(pl.multiple_of(who * GROUP, GROUP), GROUP)
            if half is None:
                return xs.at[pl.ds(0, SRCS), feat, :]
            return xs.at[pl.ds(half * (SRCS // 2), SRCS // 2), feat, :]
        if half is None:
            return xs.at[pl.ds(who * 4, 4)]
        return xs.at[pl.ds(who * 4 + half * 2, 2)]

    z_col = col + 4 - 8 * zl
    next_col, prev_col = zl * 4 + (x + 1) % 4, zl * 4 + (x + 3) % 4
    far_col = zl * 4 + (x + 2) % 4
    z_next, z_prev = next_col + 4 - 8 * zl, prev_col + 4 - 8 * zl
    z_across = far_col + 4 - 8 * zl

    def gather_0(k, ch):
        mine = block(k, ch, col)
        source = mine if k else feats.at[ch]
        remote("ag", (k, ch), 0, source, mine, z_near)
        if k:
            remote("ag", (k, ch), 3, source, mine, x_far)
        remote("ag", (k, ch), 1, source, mine, x_next)
        remote("ag", (k, ch), 2, source, mine, x_prev)

    def gather_1(k, ch):
        theirs = block(k, ch, z_col)
        arrived("ag", (k, ch), 0, theirs)
        if k:
            remote("ag", (k, ch), 6, theirs, theirs, x_far)
            remote("ag", (k, ch), 4, theirs, theirs, x_next)
            remote("ag", (k, ch), 5, theirs, theirs, x_prev)
        else:
            remote("ag", (k, ch), 3, theirs, theirs, x_next)
            remote("ag", (k, ch), 4, theirs, theirs, x_prev)

    def pass_p(k, ch, base, who):
        arrived("ag", (k, ch), base, block(k, ch, who))
        half = block(k, ch, who, 0)
        remote("ag", (k, ch), base + 4, half, half, x_next)

    def pass_m(k, ch, base, who):
        arrived("ag", (k, ch), base + 1, block(k, ch, who))
        half = block(k, ch, who, 1)
        remote("ag", (k, ch), base + 5, half, half, x_prev)

    def gather_2(k, ch):
        pass_p(k, ch, 1, prev_col)
        pass_m(k, ch, 1, next_col)

    def gather_3(k, ch):
        pass_p(k, ch, 3, z_prev)
        pass_m(k, ch, 3, z_next)

    def gather_4(k, ch):
        if k:
            who = (prev_col, next_col, far_col, z_prev, z_next, z_across)
            for i in range(6):
                arrived("ag", (k, ch), i + 1, block(k, ch, who[i]))
        else:
            arrived("ag", (k, ch), 5, block(k, ch, far_col, 0))
            arrived("ag", (k, ch), 6, block(k, ch, far_col, 1))
            arrived("ag", (k, ch), 7, block(k, ch, z_across, 0))
            arrived("ag", (k, ch), 8, block(k, ch, z_across, 1))

    def products(k, ch, q):
        xs = ref["x", (k, ch)]
        start = table[DESTS * MOST + q]
        left = jnp.concatenate([xs[table[q * MOST + j]] for j in range(MOST)], axis=1)
        right = jnp.concatenate(
            [w[jnp.minimum(start + j, SLOTS - 1)] for j in range(MOST)], axis=0
        )
        return jnp.dot(left, right, preferred_element_type=F32)

    def tail_sum(terms):
        total = None
        for term in terms:
            part = jnp.sum(term[WIDE:, :].astype(F32), axis=0, keepdims=True)
            total = part if total is None else total + part
        return total

    def add_up(terms):
        total = terms[0][:WIDE, :].astype(F32)
        for term in terms[1:]:
            total = total + term[:WIDE, :].astype(F32)
        return total

    def put(target, terms):
        target[0:WIDE, :] = add_up(terms).astype(BF16)
        if terms[0].shape[0] > WIDE:
            total = tail_sum(terms)
            high = total.astype(BF16).astype(F32)
            low = total - high
            which = lax.broadcasted_iota(jnp.int32, (TAIL, TILE), 0)
            split = jnp.where(which == 0, high, jnp.where(which == 1, low, 0.0))
            target[WIDE : WIDE + TAIL, :] = split.astype(BF16)

    def first_dest(i, side):
        zi, yi = i // 4, i % 4
        hop = (2 + 3 * yi + 3 * ((yi * (yi - 1)) // 2)) % 4
        z = (1 - zh + zi) % 2
        return (((y + hop) % 4) * 4 + z * 2 + side) * 4

    def core_copy(k, ch, pair, **how):
        give, take = ref["give", (k, ch)], ref["take", (k, ch)]
        both = pl.ds(pair * 2, 2)
        remote("core", (k, ch), pair, give.at[both], take.at[both], other_core, **how)

    def make_given(k, ch):
        give = ref["give", (k, ch)]

        def one(half, carry):
            sums = [products(k, ch, first_dest(half * 4 + e, 1 - core) + t) for e in range(4) for t in range(4)]
            for e in range(4):
                for t in range(4):
                    put(give.at[half * 4 + e, t], [sums[e * 4 + t]])
            for p in range(2):
                core_copy(k, ch, half * 2 + p, keep=False)
            return carry

        lax.fori_loop(0, 2, one, 0)
        for pair in range(4):
            core_copy(k, ch, pair, begin=False)

    def y_first(k, ch, zi, **how):
        tag, own = (k, ch), ref["own", (k, ch)]
        remote("y", tag, zi * 3, own.at[zi * 4], ref["far", tag].at[zi], y_far, **how)
        remote("y", tag, zi * 3 + 1, own.at[zi * 4 + 1], ref["near_p", tag].at[zi], y_next, **how)

    def y_second(k, ch, zi, **how):
        tag, own = (k, ch), ref["own", (k, ch)]
        remote("y", tag, zi * 3 + 2, own.at[zi * 4 + 2], ref["near_m", tag].at[zi], y_prev, **how)

    def make_own(k, ch, zi):
        own, take = ref["own", (k, ch)], ref["take", (k, ch)]

        def one(h, carry):
            pair = zi * 2 + h
            sums = [products(k, ch, first_dest(pair * 2 + e, core) + t) for e in range(2) for t in range(4)]
            arrived("core", (k, ch), pair, take.at[pl.ds(pair * 2, 2)])
            for e in range(2):
                i = pair * 2 + e
                for t in range(4):
                    put(own.at[i, t], [sums[e * 4 + t], take[i, t]])

            @pl.when(h == 0)
            def _():
                y_first(k, ch, zi, keep=False)

            @pl.when(h == 1)
            def _():
                y_second(k, ch, zi, keep=False)

            return carry

        lax.fori_loop(0, 2, one, 0)
        y_first(k, ch, zi, begin=False)
        y_second(k, ch, zi, begin=False)

    def own_0(k, ch):
        make_own(k, ch, 0)

    def own_1(k, ch):
        make_own(k, ch, 1)

    def y_terms(k, ch, zi):
        buffers = [ref[name, (k, ch)] for name in ("far", "near_p", "near_m")]
        for i, buffer in enumerate(buffers):
            arrived("y", (k, ch), zi * 3 + i, buffer.at[zi])
        own = ref["own", (k, ch)]
        return [[own[zi * 4 + 3, t]] + [buffer[zi, t] for buffer in buffers] for t in range(4)]

    def z_send(k, ch):
        tag = (k, ch)
        z_out = ref["z_out", tag]
        terms = y_terms(k, ch, 0)
        for t in range(4):
            put(z_out.at[t], terms[t])
        remote("z", tag, 0, z_out, ref["z_in", tag], z_far)

    def finish(k, ch):
        tag = (k, ch)
        z_in = ref["z_in", tag]
        sums = y_terms(k, ch, 1)
        arrived("z", tag, 0, z_in)
        for t in range(4):
            terms = sums[t] + [z_in[t]]
            if tag == (0, 0):
                scale[t] = (1.0 - TELEPORT) / (1.0 + tail_sum(terms))
            here = col * 4 + t
            old = ref["x", tag][here, 0:WIDE, :].astype(F32)
            start = ref["x", (0, ch)][here, 0:WIDE, :].astype(F32)
            new = ((add_up(terms) + old) * scale[t] + TELEPORT * start).astype(BF16)
            if k + 1 < ITERS:
                ref["x", (k + 1, ch)][here, 0:WIDE, :] = new
            else:
                for g in range(8):
                    low = g * 32 + ch * GROUP
                    out_ref[t, low : low + GROUP, :] = new[g * GROUP : (g + 1) * GROUP, :]

    def drain(k, ch):
        for copy in sends[k, ch]:
            copy.wait_send()

    def load(k, ch):
        loads[ch].wait()

    def weights(k, ch):
        w_copy.wait()

    tasks = dict(
        load=load,
        weights=weights,
        gather_0=gather_0,
        gather_1=gather_1,
        gather_2=gather_2,
        gather_3=gather_3,
        gather_4=gather_4,
        give=make_given,
        own_0=own_0,
        own_1=own_1,
        z_send=z_send,
        finish=finish,
        drain=drain,
    )
    for number, k, ch in ORDER:
        tasks[NAMES[number]](k, ch)

def on_device(features, tile_vals, tile_src, row_counts):
    feats = features.T.reshape(4, 8, SRCS, TILE).transpose(0, 2, 1, 3)
    shapes = scratch_layout()
    out = pl.pallas_call(
        functools.partial(kernel, tuple(shapes)),
        out_shape=jax.ShapeDtypeStruct((4, FEATS, TILE), BF16),
        in_specs=[pl.BlockSpec(memory_space=pltpu.SMEM)] * 2
        + [pl.BlockSpec(memory_space=pl.ANY)] * 2,
        out_specs=pl.BlockSpec(memory_space=pltpu.VMEM),
        scratch_shapes=list(shapes.values()),
        compiler_params=pltpu.CompilerParams(
            collective_id=0, has_side_effects=True, vmem_limit_bytes=58 * 2**20
        ),
        name="propagate",
    )(tile_src, row_counts, feats, tile_vals)
    return out.transpose(0, 2, 1).reshape(4 * TILE, FEATS)


def solution(mesh):
    placed = (P("row", "col"), P("row", "col", None), P("row", "col"), P("row", "col"))
    return jax.shard_map(
        on_device, mesh=mesh, in_specs=placed, out_specs=P(("row", "col"), None), check_vma=False
    )
```
